32 devices in a mesh: shot: 8 (over z, x), sub: 4 (over y, core).
Axes of the slice: x: 2, y: 2, z: 4, core: 2. Of those that a mesh axis runs over, the one named last changes fastest.
Arguments:
- courant: float32 [8, 128, 128, 128], P('shot', 'sub'), may hold values from 0.04 to 0.2
- adjoint_prev: float32 [8, 128, 128, 128], P('shot', 'sub'), may hold values from -6 to 6
- adjoint_now: float32 [8, 128, 128, 128], P('shot', 'sub'), may hold values from -6 to 6
- forward_accel: float32 [8, 4, 128, 128, 128], P('shot', None, 'sub'), may hold values from -6 to 6
- traces: float32 [8, 4, 512], P('shot'), may hold values from -24 to 24
- receivers: int32 [8, 512], P('shot'), may hold values from 0 to 2097151
- owners: int32 [8, 4, 16, 1], P('shot', 'sub'), may hold values from 0 to 7; in each aligned block of 16 rows (0 to 15, 16 to 31, ..., all dimensions but the last counted through in order) at most 2 rows name the same one
- tile_slot: int32 [8, 4, 16], P('shot', 'sub'), may hold values from 0 to 7
Outputs:
- smoothed: float32 [64, 128, 8, 128], P('shot', 'sub')
- adjoint_last: float32 [8, 128, 128, 128], P('shot', 'sub')
The draws below stay inside these ranges and needn't reach their ends.
Inputs may be any that keep to these rules, and one draw needn't show every extreme that they name: `owners`: among the 16 blocks of one device at most 2 name the same owner, and in some device's blocks one owner is named by exactly 2.
All inputs are finite; a program needn't handle non-finite values.
Results may differ from the reference program's by a relative error of at most 0.00013.
Values sent between devices are 32-bit elements; how exact they have to be, the bound alone decides.
A program may use at most 128 MiB of HBM per device.

```python
import math
import jax
import jax.numpy as jnp
import numpy as np
from jax import lax

ZD = 32
AX = 128
AY = 128
TX = 8
TILES_OWN = 8
CAP = 2
STEPS = 4
NREC = 512
Z = 128
KB = 16
NT = 64
N_SHOT = 8
N_SUB = 4


def with_ends(array, own_key, least, largest):
    index_at = [jax.random.randint(jax.random.fold_in(own_key, axis), (), 0, length) for axis, length in enumerate(array.shape)]
    main_axis = array.shape.index(max(array.shape))
    neighbour = index_at[:main_axis] + [(index_at[main_axis] + 1) % array.shape[main_axis]] + index_at[main_axis + 1:]
    return array.at[tuple(index_at)].set(least).at[tuple(neighbour)].set(largest)


def block_scale(own_key, dims, shards, smallest, high):
    level, own = 1.0, jax.random.fold_in(own_key, 6)
    for position, blocks in shards:
        steps = jnp.exp(jax.random.uniform(jax.random.fold_in(own, position), (blocks,), jnp.float32, smallest / len(shards), high / len(shards)))
        level = level * jnp.repeat(steps, dims[position] // blocks).reshape([-1 if axis == position else 1 for axis in range(len(dims))])
    return level


def routed_block(rng, own, number, rows, amount, top, bound, skew):
    sequence = jax.random.permutation(rng, amount)
    crowded, ordinary = load_shares(amount, rows * top, bound, skew, True), load_shares(amount, rows * top, bound, skew, False)
    places = jnp.arange(amount)

    def named(tallies, rotation):
        used = int((tallies > 0).sum())
        fixed = max(1, used // 4)
        moved = fixed + (places - fixed + rotation * (used - fixed)) % max(1, amount - fixed)
        return jnp.zeros((amount,), jnp.int32).at[sequence[jnp.where(places < fixed, places, moved)]].set(jnp.asarray(tallies, jnp.int32))

    tallies = jnp.where(number % 4 == 0, named(crowded, number // 4), named(ordinary, number - number // 4 - 1))
    mixed = jax.random.permutation(jax.random.fold_in(own, 3), amount)
    donor, sink = mixed[0:amount // 2 * 2:2], mixed[1:amount // 2 * 2:2]
    slack = jnp.minimum(tallies[donor] - 1, bound - tallies[sink]) // 2
    slack = jnp.where((donor == sequence[0]) | (sink == sequence[0]) | (tallies[sink] == 0), 0, jnp.maximum(slack, 0))
    moved = jax.random.randint(jax.random.fold_in(own, 4), (amount // 2,), 0, 1 << 20) % (slack + 1)
    tallies = tallies.at[donor].add(-moved).at[sink].add(moved)
    labels = jnp.searchsorted(jnp.cumsum(tallies), jnp.arange(rows * top), side="right").astype(jnp.int32)
    grid = labels.reshape(top, rows).T
    grid = grid[jax.random.permutation(jax.random.fold_in(own, 1), rows)]
    rotation = jax.random.randint(jax.random.fold_in(own, 2), (rows, 1), 0, top)
    return jnp.take_along_axis(grid, (jnp.arange(top)[None, :] + rotation) % top, axis=1)


def load_shares(number_of, total, limit, lean, full):
    weights = [(1 << 20) // math.isqrt(rank ** lean) + 1 for rank in range(1, number_of + 1)]
    largest = limit if full else min(limit, max(-(-total // number_of), total * weights[0] // sum(weights)))
    least = 1 if total - largest >= number_of - 1 else 0
    counts, spare = [largest] + [least] * (number_of - 1), total - largest - least * (number_of - 1)
    while spare > 0:
        free = [i for i in range(1, number_of) if counts[i] < largest] or [i for i in range(1, number_of) if counts[i] < limit]
        pool, left = sum([weights[i] for i in free]), spare
        for i in free:
            extra = min(limit - counts[i], max(1, left * weights[i] // pool), spare)
            counts[i] = counts[i] + extra
            spare = spare - extra
    return np.array(counts)


def centred(key, extent, scale, bound, split=(), kind=jnp.bfloat16):
    factor_of = block_scale(key, extent, split, -0.22, 0.18) if split else 1.0
    result = jax.random.normal(key, extent, jnp.float32) * scale * factor_of
    return jnp.minimum(jnp.maximum(result, -bound), bound).astype(kind)


def setup_inputs(seed: int = 0) -> dict:
    splits = jax.random.split(jax.random.key(seed), 9)
    courant = jnp.clip(jnp.exp(math.log(0.2) - 1.609438 * jax.random.uniform(splits[0], (N_SHOT, Z, AX, AY), jnp.float32) ** block_scale(splits[0], (N_SHOT, Z, AX, AY), ((0, 8), (1, 4)), -0.2, 0.2)), 0.04, 0.2)
    adjoint_prev = centred(splits[1], (N_SHOT, Z, AX, AY), 1.0, 6.0, ((0, 8), (1, 4)), jnp.float32)
    adjoint_now = centred(splits[2], (N_SHOT, Z, AX, AY), 1.0, 6.0, ((0, 8), (1, 4)), jnp.float32)
    forward_accel = centred(splits[3], (N_SHOT, STEPS, Z, AX, AY), 1.0, 6.0, ((0, 8), (2, 4)), jnp.float32)
    traces = centred(splits[4], (N_SHOT, STEPS, NREC), 4.0, 24.0, ((0, 8),), jnp.float32)
    receivers = with_ends(jax.random.randint(splits[5], (N_SHOT, NREC), 0, Z * AX * AY), jax.random.fold_in(splits[5], 1), 0, (Z * AX * AY) - 1).astype(jnp.int32)
    owners_keys = jax.random.split(jax.random.fold_in(splits[6], 1), N_SHOT * N_SUB * KB // KB)
    owners_turns = jax.random.permutation(jax.random.fold_in(splits[6], 3), N_SHOT * N_SUB * KB // KB)
    owners = jax.vmap(lambda own, number: routed_block(jax.random.fold_in(splits[6], 2), own, number, KB, N_SHOT, 1, CAP, 2))(owners_keys, owners_turns).reshape((N_SHOT, N_SUB, KB, 1))
    tile_slot = with_ends(jax.random.randint(splits[7], (N_SHOT, N_SUB, KB), 0, TILES_OWN), jax.random.fold_in(splits[7], 1), 0, TILES_OWN - 1).astype(jnp.int32)
    return {"courant": courant, "adjoint_prev": adjoint_prev, "adjoint_now": adjoint_now, "forward_accel": forward_accel, "traces": traces, "receivers": receivers, "owners": owners, "tile_slot": tile_slot}


stencil_weights = (-205.0 / 72.0, 8.0 / 5.0, -1.0 / 5.0, 8.0 / 315.0, -1.0 / 560.0)


def laplace_eight(padded, depth_len, rows_x, cols_y):
    centre = padded[4:4 + depth_len, 4:4 + rows_x, 4:4 + cols_y]
    summed = 3.0 * stencil_weights[0] * centre
    for distance in range(1, 5):
        factor = stencil_weights[distance]
        pairs = padded[4 + distance:4 + distance + depth_len, 4:4 + rows_x, 4:4 + cols_y]
        pairs = pairs + padded[4 - distance:4 - distance + depth_len, 4:4 + rows_x, 4:4 + cols_y]
        pairs = pairs + padded[4:4 + depth_len, 4 + distance:4 + distance + rows_x, 4:4 + cols_y]
        pairs = pairs + padded[4:4 + depth_len, 4 - distance:4 - distance + rows_x, 4:4 + cols_y]
        pairs = pairs + padded[4:4 + depth_len, 4:4 + rows_x, 4 + distance:4 + distance + cols_y]
        pairs = pairs + padded[4:4 + depth_len, 4:4 + rows_x, 4 - distance:4 - distance + cols_y]
        summed = summed + factor * pairs
    return summed


def band_matrix(depth_len, band_reach):
    row_ids = jnp.arange(depth_len)[:, None]
    col_ids = jnp.arange(depth_len)[None, :]
    distance = (row_ids - col_ids).astype(jnp.float32)
    weights = jnp.where(jnp.abs(row_ids - col_ids) <= band_reach, jnp.exp(-(2.0 * distance / band_reach) ** 2), 0.0)
    return weights / jnp.sum(weights, axis=1, keepdims=True)


def propagate(inputs):
    speed, previous, current, accel, trace, receiver = inputs
    gradient = jnp.zeros_like(current)
    for time_step in range(STEPS):
        padded = jnp.pad(current, 4)
        advanced = 2.0 * current - previous + speed * laplace_eight(padded, Z, AX, AY)
        advanced = advanced.reshape(-1).at[receiver].add(trace[time_step]).reshape(current.shape)
        gradient = gradient + advanced * accel[time_step]
        previous, current = current, advanced
    return current, gradient


def slab_sum(blocks, tile_ids):
    return jax.ops.segment_sum(blocks, tile_ids, num_segments=NT)


def reference(courant, adjoint_prev, adjoint_now, forward_accel, traces, receivers, owners, tile_slot):
    adjoint_last, gradients = lax.map(propagate, (courant, adjoint_prev, adjoint_now, forward_accel, traces, receivers))
    blocks = gradients.reshape(N_SHOT, N_SUB, ZD, KB, TX, AY).transpose(1, 0, 3, 2, 4, 5).reshape(N_SUB, N_SHOT * KB, ZD, TX, AY)
    tile_ids = (owners[:, :, :, 0] * TILES_OWN + tile_slot).transpose(1, 0, 2).reshape(N_SUB, N_SHOT * KB).astype(jnp.int32)
    per_slab = jax.vmap(slab_sum)(blocks, tile_ids)
    model = per_slab.transpose(1, 0, 2, 3, 4).reshape(NT, Z, TX, AY)
    smoothed = jnp.einsum('ij,tjxy->tixy', band_matrix(Z, ZD), model, precision=lax.Precision.HIGHEST)
    return smoothed, adjoint_last
```

```python
import functools

import jax
import jax.numpy as jnp
from jax import lax
from jax.experimental import pallas as pl
from jax.experimental.pallas import tpu as pltpu
from jax.sharding import PartitionSpec as P

TX = 8
TILES_OWN = 8
CAP = 2
HALO = 4
PAD = 8
MESH = pl.DeviceIdType.MESH

stencil_weights = (-205.0 / 72.0, 8.0 / 5.0, -1.0 / 5.0, 8.0 / 315.0, -1.0 / 560.0)


def prepare_kernel(slab_cells, cols_y, rec_ref, tr_ref, own_ref, slot_ref, src_ref, inv_ref, ids_ref, count_ref):
    steps = src_ref.shape[0]
    zrows = 256

    def zero(i, _):
        src_ref[:, pl.ds(pl.multiple_of(i * zrows, zrows), zrows), :] = jnp.zeros(
            (steps, zrows, cols_y), jnp.float32
        )
        return 0

    lax.fori_loop(0, src_ref.shape[1] // zrows, zero, 0)
    base = lax.axis_index("sub") * slab_cells
    lane = lax.broadcasted_iota(jnp.int32, (1, cols_y), 1)

    def add(r, _):
        off = rec_ref[0, r] - base

        @pl.when((off >= 0) & (off < slab_cells))
        def _():
            row = lax.div(off, cols_y)
            hit = lane == lax.rem(off, cols_y)
            for t in range(steps):
                src_ref[t, pl.ds(row, 1), :] += jnp.where(hit, tr_ref[0, t, r], 0.0)

        return 0

    lax.fori_loop(0, rec_ref.shape[1], add, 0, unroll=4)

    ids_ref[...] = jnp.full(ids_ref.shape, -1, jnp.int32)
    for i in range(count_ref.shape[0]):
        count_ref[i] = 0
    for i in range(inv_ref.shape[0]):
        inv_ref[i] = 0
    for k in range(slot_ref.shape[2]):
        owner = own_ref[0, 0, k, 0]
        place = owner * CAP + count_ref[owner]
        count_ref[owner] = count_ref[owner] + 1
        inv_ref[place] = k
        ids_ref[pl.ds(place, 1)] = jnp.full((1,) + ids_ref.shape[1:], slot_ref[0, 0, k], jnp.int32)


def wave_kernel(
    n_sub, inv_ref, cour_hbm, prev_hbm, now_hbm, acc_hbm, src_hbm,
    last_hbm, send_hbm,
    buf, cour, acc, src, grad, packed,
    lsem, tsem, hsend, hrecv, psem, osem,
):
    me = lax.axis_index("sub")
    steps, depth, rows, cols = acc.shape
    lo, hi = HALO, HALO + depth
    inner = pl.ds(PAD, rows)

    local = [
        pltpu.make_async_copy(now_hbm.at[0], buf.at[0, lo:hi, inner, :], lsem.at[0]),
        pltpu.make_async_copy(prev_hbm.at[0], buf.at[1, lo:hi, inner, :], lsem.at[1]),
        pltpu.make_async_copy(cour_hbm.at[0], cour, lsem.at[2]),
    ]
    per_step = [
        (
            pltpu.make_async_copy(src_hbm.at[t], src.at[t], tsem.at[t, 0]),
            pltpu.make_async_copy(acc_hbm.at[0, t], acc.at[t], tsem.at[t, 1]),
        )
        for t in range(steps)
    ]
    for c in local:
        c.start()
    for t in range(steps):
        for c in per_step[t]:
            c.start()

    for b in range(2):
        buf[b, :, 0:PAD, :] = jnp.zeros((depth + 2 * HALO, PAD, cols), jnp.float32)
        buf[b, :, PAD + rows :, :] = jnp.zeros((depth + 2 * HALO, PAD, cols), jnp.float32)
        buf[b, 0:lo, inner, :] = jnp.zeros((HALO, rows, cols), jnp.float32)
        buf[b, hi:, inner, :] = jnp.zeros((HALO, rows, cols), jnp.float32)

    has_up, has_down = me > 0, me < n_sub - 1
    barrier = pltpu.get_barrier_semaphore()

    @pl.when(has_up)
    def _():
        pl.semaphore_signal(barrier, inc=1, device_id={"sub": me - 1}, device_id_type=MESH)

    @pl.when(has_down)
    def _():
        pl.semaphore_signal(barrier, inc=1, device_id={"sub": me + 1}, device_id_type=MESH)

    pl.semaphore_wait(barrier, jnp.minimum(me, 1) + jnp.minimum(n_sub - 1 - me, 1))

    def halos(t):
        b = t % 2
        if t == 0:
            first, final = now_hbm.at[0, 0:HALO], now_hbm.at[0, depth - HALO : depth]
        else:
            first = buf.at[b, lo : lo + HALO, inner, :]
            final = buf.at[b, hi - HALO : hi, inner, :]
        up = pltpu.make_async_remote_copy(
            src_ref=first, dst_ref=buf.at[b, hi : hi + HALO, inner, :],
            send_sem=hsend.at[t, 0], recv_sem=hrecv.at[t, 0],
            device_id={"sub": me - 1}, device_id_type=MESH,
        )
        down = pltpu.make_async_remote_copy(
            src_ref=final, dst_ref=buf.at[b, 0:HALO, inner, :],
            send_sem=hsend.at[t, 1], recv_sem=hrecv.at[t, 1],
            device_id={"sub": me + 1}, device_id_type=MESH,
        )
        return up, down

    def start_halos(t):
        up, down = halos(t)

        @pl.when(has_up)
        def _():
            up.start()

        @pl.when(has_down)
        def _():
            down.start()

    def wait_halos(t):
        up, down = halos(t)

        @pl.when(has_up)
        def _():
            up.wait_send()
            down.wait_recv()

        @pl.when(has_down)
        def _():
            down.wait_send()
            up.wait_recv()

    start_halos(0)

    lane = lax.broadcasted_iota(jnp.int32, (TX, cols), 1)
    from_left = [None] + [jnp.where(lane >= d, stencil_weights[d], 0.0) for d in range(1, 5)]
    from_right = [None] + [jnp.where(lane < cols - d, stencil_weights[d], 0.0) for d in range(1, 5)]

    def advance(t, chunks):
        cur, nxt = t % 2, (t + 1) % 2

        def block(xb, _):
            x0 = pl.multiple_of(xb * TX, TX)
            own = pl.ds(x0, TX)
            here = pl.ds(pl.multiple_of(x0 + PAD, TX), TX)
            for za, zb in chunks:
                col = {z: buf[cur, z + HALO, here, :] for z in range(za - 4, zb + 4)}
                for z in range(za, zb):
                    c = col[z]
                    lap = (3.0 * stencil_weights[0]) * c
                    for d in range(1, 5):
                        pair = (col[z + d] + col[z - d]) + (
                            buf[cur, z + HALO, pl.ds(x0 + (PAD + d), TX), :]
                            + buf[cur, z + HALO, pl.ds(x0 + (PAD - d), TX), :]
                        )
                        lap = lap + stencil_weights[d] * pair
                        lap = lap + from_left[d] * pltpu.roll(c, d, 1)
                        lap = lap + from_right[d] * pltpu.roll(c, cols - d, 1)
                    adv = (2.0 * c - buf[nxt, z + HALO, here, :]) + (
                        cour[z, own, :] * lap + src[t, z, own, :]
                    )
                    buf[nxt, z + HALO, here, :] = adv
                    g = adv * acc[t, z, own, :]
                    grad[xb, z] = g if t == 0 else grad[xb, z] + g
            return 0

        lax.fori_loop(0, rows // TX, block, 0)

    for c in local:
        c.wait()
    mid = [(z, min(z + 8, depth - HALO)) for z in range(HALO, depth - HALO, 8)]
    for t in range(steps):
        for c in per_step[t]:
            c.wait()
        advance(t, mid)
        wait_halos(t)
        advance(t, [(0, HALO), (depth - HALO, depth)])
        if t + 1 < steps:
            start_halos(t + 1)

    out = pltpu.make_async_copy(buf.at[steps % 2, lo:hi, inner, :], last_hbm.at[0], osem)
    out.start()
    places = packed.shape[0]

    def pack(p, _):
        packed[p] = grad[inv_ref[p]]
        pltpu.make_async_copy(packed.at[p], send_hbm.at[p], psem.at[p]).start()
        return 0

    lax.fori_loop(0, places, pack, 0)

    def drain(p, _):
        pltpu.make_async_copy(packed.at[p], send_hbm.at[p], psem.at[p]).wait()
        return 0

    lax.fori_loop(0, places, drain, 0)
    out.wait()


def tile_kernel(
    n_shot, n_sub, send_hbm, ids_hbm, out_hbm,
    recv, rids, tiles, smooth,
    lsem, dsend, drecv, isend, irecv, nsend, nrecv, osem,
):
    shot, sub = lax.axis_index("shot"), lax.axis_index("sub")
    depth, cols = recv.shape[1], recv.shape[3]
    has_up, has_down = sub > 0, sub < n_sub - 1
    barrier = pltpu.get_barrier_semaphore()
    for i in range(1, n_shot):
        pl.semaphore_signal(
            barrier, inc=1, device_id={"shot": lax.rem(shot + i, n_shot)}, device_id_type=MESH
        )

    @pl.when(has_up)
    def _():
        pl.semaphore_signal(barrier, inc=1, device_id={"sub": sub - 1}, device_id_type=MESH)

    @pl.when(has_down)
    def _():
        pl.semaphore_signal(barrier, inc=1, device_id={"sub": sub + 1}, device_id_type=MESH)

    near = jnp.minimum(sub, 1) + jnp.minimum(n_sub - 1 - sub, 1)
    pl.semaphore_wait(barrier, n_shot - 1 + near)

    def part(i):
        return pl.ds(pl.multiple_of(i * CAP, CAP), CAP)

    copies = []
    for i in range(1, n_shot):
        peer = lax.rem(shot + i, n_shot)
        for src, dst, ss, rs in ((ids_hbm, rids, isend, irecv), (send_hbm, recv, dsend, drecv)):
            copies.append(
                pltpu.make_async_remote_copy(
                    src_ref=src.at[part(peer)], dst_ref=dst.at[CAP * i : CAP * (i + 1)],
                    send_sem=ss.at[i], recv_sem=rs.at[i],
                    device_id={"shot": peer}, device_id_type=MESH,
                )
            )
    for c in copies:
        c.start()
    mine = [
        pltpu.make_async_copy(send_hbm.at[part(shot)], recv.at[0:CAP], lsem.at[0]),
        pltpu.make_async_copy(ids_hbm.at[part(shot)], rids.at[0:CAP], lsem.at[1]),
    ]
    for c in mine:
        c.start()

    band_i = lax.broadcasted_iota(jnp.int32, (depth, 3 * depth), 0)
    band_j = lax.broadcasted_iota(jnp.int32, (depth, 3 * depth), 1) - depth
    there = band_j + sub * depth
    gap = band_i - band_j
    ratio = 2.0 * gap.astype(jnp.float32) / depth
    valid = (jnp.abs(gap) <= depth) & (there >= 0) & (there < n_sub * depth)
    band = jnp.where(valid, jnp.exp(-(ratio * ratio)), 0.0)
    band = band / jnp.sum(band, axis=1, keepdims=True)

    @pl.when(jnp.logical_not(has_up))
    def _():
        tiles[:, 0] = jnp.zeros((TILES_OWN, depth * TX, cols), jnp.float32)

    @pl.when(jnp.logical_not(has_down))
    def _():
        tiles[:, 2] = jnp.zeros((TILES_OWN, depth * TX, cols), jnp.float32)

    def gather(blocks, fresh):
        def layer(z, _):
            rows = pl.ds(pl.multiple_of(z * TX, TX), TX)
            data = [recv[p, z] for p in blocks]
            for t in range(TILES_OWN):
                total = None if fresh else tiles[t, 1, rows, :]
                for p, v in zip(blocks, data):
                    term = jnp.where(rids[p] == t, v, 0.0)
                    total = term if total is None else total + term
                tiles[t, 1, rows, :] = total
            return 0

        lax.fori_loop(0, depth, layer, 0)

    for c in mine:
        c.wait()
    gather(range(CAP), True)
    for i in range(1, n_shot):
        copies[2 * i - 2].wait()
        copies[2 * i - 1].wait()
        gather(range(CAP * i, CAP * (i + 1)), False)

    def edge(t):
        up = pltpu.make_async_remote_copy(
            src_ref=tiles.at[t, 1], dst_ref=tiles.at[t, 2],
            send_sem=nsend.at[t, 0], recv_sem=nrecv.at[t, 0],
            device_id={"sub": sub - 1}, device_id_type=MESH,
        )
        down = pltpu.make_async_remote_copy(
            src_ref=tiles.at[t, 1], dst_ref=tiles.at[t, 0],
            send_sem=nsend.at[t, 1], recv_sem=nrecv.at[t, 1],
            device_id={"sub": sub + 1}, device_id_type=MESH,
        )
        return up, down

    def start_edge(t, _):
        up, down = edge(t)

        @pl.when(has_up)
        def _():
            up.start()

        @pl.when(has_down)
        def _():
            down.start()

        return 0

    lax.fori_loop(0, TILES_OWN, start_edge, 0)

    def finish(t, _):
        up, down = edge(t)

        @pl.when(has_up)
        def _():
            up.wait_send()
            down.wait_recv()

        @pl.when(has_down)
        def _():
            down.wait_send()
            up.wait_recv()

        for x in range(TX):
            pencil = jnp.concatenate(
                [tiles[t, s, pl.ds(x, depth, stride=TX), :] for s in range(3)], axis=0
            )
            smooth[t, pl.ds(x, depth, stride=TX), :] = jnp.dot(
                band, pencil, precision=lax.Precision.HIGHEST, preferred_element_type=jnp.float32
            )
        pltpu.make_async_copy(smooth.at[t], out_hbm.at[t], osem.at[t]).start()
        return 0

    lax.fori_loop(0, TILES_OWN, finish, 0)

    def drain(t, _):
        pltpu.make_async_copy(smooth.at[t], out_hbm.at[t], osem.at[t]).wait()
        return 0

    lax.fori_loop(0, TILES_OWN, drain, 0)


def body(courant, adjoint_prev, adjoint_now, forward_accel, traces, receivers, owners, tile_slot):
    n_sub = lax.axis_size("sub")
    n_shot = lax.axis_size("shot")
    _, steps, depth, rows, cols = forward_accel.shape
    places = n_shot * CAP
    f32 = jnp.float32
    smem = pl.BlockSpec(memory_space=pltpu.SMEM)
    vmem = pl.BlockSpec(memory_space=pltpu.VMEM)
    hbm = pl.BlockSpec(memory_space=pl.ANY)

    source, inverse, ids = pl.pallas_call(
        functools.partial(prepare_kernel, depth * rows * cols, cols),
        out_shape=(
            jax.ShapeDtypeStruct((steps, depth * rows, cols), f32),
            jax.ShapeDtypeStruct((places,), jnp.int32),
            jax.ShapeDtypeStruct((places, 8, cols), jnp.int32),
        ),
        in_specs=[smem] * 4,
        out_specs=(vmem, smem, vmem),
        scratch_shapes=[pltpu.SMEM((n_shot,), jnp.int32)],
        compiler_params=pltpu.CompilerParams(vmem_limit_bytes=32 * 2**20),
        name="prepare",
    )(receivers, traces, owners, tile_slot)
    source = source.reshape(steps, depth, rows, cols)

    last, send = pl.pallas_call(
        functools.partial(wave_kernel, n_sub),
        out_shape=(
            jax.ShapeDtypeStruct((1, depth, rows, cols), f32),
            jax.ShapeDtypeStruct((places, depth, TX, cols), f32),
        ),
        in_specs=[smem] + [hbm] * 5,
        out_specs=(hbm, hbm),
        scratch_shapes=[
            pltpu.VMEM((2, depth + 2 * HALO, rows + 2 * PAD, cols), f32),
            pltpu.VMEM((depth, rows, cols), f32),
            pltpu.VMEM((steps, depth, rows, cols), f32),
            pltpu.VMEM((steps, depth, rows, cols), f32),
            pltpu.VMEM((rows // TX, depth, TX, cols), f32),
            pltpu.VMEM((places, depth, TX, cols), f32),
            pltpu.SemaphoreType.DMA((3,)),
            pltpu.SemaphoreType.DMA((steps, 2)),
            pltpu.SemaphoreType.DMA((steps, 2)),
            pltpu.SemaphoreType.DMA((steps, 2)),
            pltpu.SemaphoreType.DMA((places,)),
            pltpu.SemaphoreType.DMA,
        ],
        compiler_params=pltpu.CompilerParams(
            collective_id=0, has_side_effects=True, vmem_limit_bytes=48 * 2**20
        ),
        name="wave",
    )(inverse, courant, adjoint_prev, adjoint_now, forward_accel, source)

    smoothed = pl.pallas_call(
        functools.partial(tile_kernel, n_shot, n_sub),
        out_shape=jax.ShapeDtypeStruct((TILES_OWN, depth * TX, cols), f32),
        in_specs=[hbm, hbm],
        out_specs=hbm,
        scratch_shapes=[
            pltpu.VMEM((places, depth, TX, cols), f32),
            pltpu.VMEM((places, 8, cols), jnp.int32),
            pltpu.VMEM((TILES_OWN, 3, depth * TX, cols), f32),
            pltpu.VMEM((TILES_OWN, depth * TX, cols), f32),
            pltpu.SemaphoreType.DMA((2,)),
            pltpu.SemaphoreType.DMA((n_shot,)),
            pltpu.SemaphoreType.DMA((n_shot,)),
            pltpu.SemaphoreType.DMA((n_shot,)),
            pltpu.SemaphoreType.DMA((n_shot,)),
            pltpu.SemaphoreType.DMA((TILES_OWN, 2)),
            pltpu.SemaphoreType.DMA((TILES_OWN, 2)),
            pltpu.SemaphoreType.DMA((TILES_OWN,)),
        ],
        compiler_params=pltpu.CompilerParams(
            collective_id=1, has_side_effects=True, vmem_limit_bytes=32 * 2**20
        ),
        name="tiles",
    )(send, ids)
    return (smoothed.reshape(TILES_OWN, depth, TX, cols), last)


def solution(mesh):
    placed = (
        P("shot", "sub", None, None),
        P("shot", "sub", None, None),
        P("shot", "sub", None, None),
        P("shot", None, "sub", None, None),
        P("shot", None, None),
        P("shot", None),
        P("shot", "sub", None, None),
        P("shot", "sub", None),
    )
    return jax.shard_map(
        body,
        mesh=mesh,
        in_specs=placed,
        out_specs=(P("shot", "sub", None, None), P("shot", "sub", None, None)),
        check_vma=False,
    )
```

```python
import functools

import jax
import jax.numpy as jnp
from jax import lax
from jax.experimental import pallas as pl
from jax.experimental.pallas import tpu as pltpu
from jax.sharding import PartitionSpec as P

TX = 8
TILES_OWN = 8
CAP = 2
HALO = 4
PAD = 8
MESH = pl.DeviceIdType.MESH

stencil_weights = (-205.0 / 72.0, 8.0 / 5.0, -1.0 / 5.0, 8.0 / 315.0, -1.0 / 560.0)


def prepare_kernel(slab_cells, cols_y, rec_ref, tr_ref, own_ref, slot_ref, *refs):
    *src_refs, inv_ref, ids_ref, count_ref = refs
    zrows = 256

    def zero(i, _):
        for ref in src_refs:
            ref[pl.ds(pl.multiple_of(i * zrows, zrows), zrows), :] = jnp.zeros(
                (zrows, cols_y), jnp.float32
            )
        return 0

    lax.fori_loop(0, src_refs[0].shape[0] // zrows, zero, 0)
    base = lax.axis_index("sub") * slab_cells
    lane = lax.broadcasted_iota(jnp.int32, (1, cols_y), 1)

    def add(r, _):
        off = rec_ref[0, r] - base

        @pl.when((off >= 0) & (off < slab_cells))
        def _():
            row = lax.div(off, cols_y)
            hit = lane == lax.rem(off, cols_y)
            old = [ref[pl.ds(row, 1), :] for ref in src_refs]
            for t, ref in enumerate(src_refs):
                ref[pl.ds(row, 1), :] = old[t] + jnp.where(hit, tr_ref[0, t, r], 0.0)

        return 0

    lax.fori_loop(0, rec_ref.shape[1], add, 0, unroll=4)

    ids_ref[...] = jnp.full(ids_ref.shape, -1, jnp.int32)
    for i in range(count_ref.shape[0]):
        count_ref[i] = 0
    for i in range(inv_ref.shape[0]):
        inv_ref[i] = 0
    for k in range(slot_ref.shape[2]):
        owner = own_ref[0, 0, k, 0]
        place = owner * CAP + count_ref[owner]
        count_ref[owner] = count_ref[owner] + 1
        inv_ref[place] = k
        ids_ref[pl.ds(place, 1)] = jnp.full((1,) + ids_ref.shape[1:], slot_ref[0, 0, k], jnp.int32)


def wave_kernel(
    n_sub, inv_ref, cour_hbm, prev_hbm, now_hbm, acc_hbm, *refs,
):
    steps = acc_hbm.shape[1]
    src = refs[:steps]
    last_hbm, send_hbm, buf, cour, acc, grad, packed, lsem, tsem, hsend, hrecv, psem, osem = refs[steps:]
    me = lax.axis_index("sub")
    steps, depth, rows, cols = acc.shape
    lo, hi = HALO, HALO + depth
    inner = pl.ds(PAD, rows)

    local = [
        pltpu.make_async_copy(now_hbm.at[0], buf.at[0, lo:hi, inner, :], lsem.at[0]),
        pltpu.make_async_copy(prev_hbm.at[0], buf.at[1, lo:hi, inner, :], lsem.at[1]),
        pltpu.make_async_copy(cour_hbm.at[0], cour, lsem.at[2]),
    ]
    per_step = [
        (pltpu.make_async_copy(acc_hbm.at[0, t], acc.at[t], tsem.at[t]),)
        for t in range(steps)
    ]
    for c in local:
        c.start()
    for t in range(steps):
        for c in per_step[t]:
            c.start()

    for b in range(2):
        buf[b, :, 0:PAD, :] = jnp.zeros((depth + 2 * HALO, PAD, cols), jnp.float32)
        buf[b, :, PAD + rows :, :] = jnp.zeros((depth + 2 * HALO, PAD, cols), jnp.float32)
        buf[b, 0:lo, inner, :] = jnp.zeros((HALO, rows, cols), jnp.float32)
        buf[b, hi:, inner, :] = jnp.zeros((HALO, rows, cols), jnp.float32)

    has_up, has_down = me > 0, me < n_sub - 1
    barrier = pltpu.get_barrier_semaphore()

    @pl.when(has_up)
    def _():
        pl.semaphore_signal(barrier, inc=1, device_id={"sub": me - 1}, device_id_type=MESH)

    @pl.when(has_down)
    def _():
        pl.semaphore_signal(barrier, inc=1, device_id={"sub": me + 1}, device_id_type=MESH)

    pl.semaphore_wait(barrier, jnp.minimum(me, 1) + jnp.minimum(n_sub - 1 - me, 1))

    def halos(t):
        b = t % 2
        if t == 0:
            first, final = now_hbm.at[0, 0:HALO], now_hbm.at[0, depth - HALO : depth]
        else:
            first = buf.at[b, lo : lo + HALO, inner, :]
            final = buf.at[b, hi - HALO : hi, inner, :]
        up = pltpu.make_async_remote_copy(
            src_ref=first, dst_ref=buf.at[b, hi : hi + HALO, inner, :],
            send_sem=hsend.at[t, 0], recv_sem=hrecv.at[t, 0],
            device_id={"sub": me - 1}, device_id_type=MESH,
        )
        down = pltpu.make_async_remote_copy(
            src_ref=final, dst_ref=buf.at[b, 0:HALO, inner, :],
            send_sem=hsend.at[t, 1], recv_sem=hrecv.at[t, 1],
            device_id={"sub": me + 1}, device_id_type=MESH,
        )
        return up, down

    def start_halos(t):
        up, down = halos(t)

        @pl.when(has_up)
        def _():
            up.start()

        @pl.when(has_down)
        def _():
            down.start()

    def wait_halos(t):
        up, down = halos(t)

        @pl.when(has_up)
        def _():
            up.wait_send()
            down.wait_recv()

        @pl.when(has_down)
        def _():
            down.wait_send()
            up.wait_recv()

    start_halos(0)

    lane = lax.broadcasted_iota(jnp.int32, (TX, cols), 1)
    from_left = [None] + [jnp.where(lane >= d, stencil_weights[d], 0.0) for d in range(1, 5)]
    from_right = [None] + [jnp.where(lane < cols - d, stencil_weights[d], 0.0) for d in range(1, 5)]

    def advance(t, chunks):
        cur, nxt = t % 2, (t + 1) % 2

        def block(xb, _):
            x0 = pl.multiple_of(xb * TX, TX)
            own = pl.ds(x0, TX)
            here = pl.ds(pl.multiple_of(x0 + PAD, TX), TX)
            for za, zb in chunks:
                col = {z: buf[cur, z + HALO, here, :] for z in range(za - 4, zb + 4)}
                for z in range(za, zb):
                    c = col[z]
                    lap = (3.0 * stencil_weights[0]) * c
                    for d in range(1, 5):
                        pair = (col[z + d] + col[z - d]) + (
                            buf[cur, z + HALO, pl.ds(x0 + (PAD + d), TX), :]
                            + buf[cur, z + HALO, pl.ds(x0 + (PAD - d), TX), :]
                        )
                        lap = lap + stencil_weights[d] * pair
                        lap = lap + from_left[d] * pltpu.roll(c, d, 1)
                        lap = lap + from_right[d] * pltpu.roll(c, cols - d, 1)
                    adv = (2.0 * c - buf[nxt, z + HALO, here, :]) + (
                        cour[z, own, :] * lap + src[t][z, own, :]
                    )
                    buf[nxt, z + HALO, here, :] = adv
                    g = adv * acc[t, z, own, :]
                    grad[xb, z] = g if t == 0 else grad[xb, z] + g
            return 0

        lax.fori_loop(0, rows // TX, block, 0)

    for c in local:
        c.wait()
    mid = [(z, min(z + 8, depth - HALO)) for z in range(HALO, depth - HALO, 8)]
    for t in range(steps):
        for c in per_step[t]:
            c.wait()
        advance(t, mid)
        wait_halos(t)
        advance(t, [(0, HALO), (depth - HALO, depth)])
        if t + 1 < steps:
            start_halos(t + 1)

    out = pltpu.make_async_copy(buf.at[steps % 2, lo:hi, inner, :], last_hbm.at[0], osem)
    out.start()
    places = packed.shape[0]

    def pack(p, _):
        packed[p] = grad[inv_ref[p]]
        pltpu.make_async_copy(packed.at[p], send_hbm.at[p], psem.at[p]).start()
        return 0

    lax.fori_loop(0, places, pack, 0)

    def drain(p, _):
        pltpu.make_async_copy(packed.at[p], send_hbm.at[p], psem.at[p]).wait()
        return 0

    lax.fori_loop(0, places, drain, 0)
    out.wait()


def tile_kernel(
    n_shot, n_sub, send_hbm, ids_hbm, out_hbm,
    recv, rids, near, nids, tiles, smooth,
    lsem, dsend, drecv, isend, irecv, nsend, nrecv, osem,
):
    shot, sub = lax.axis_index("shot"), lax.axis_index("sub")
    depth, cols = recv.shape[1], recv.shape[3]
    has_up, has_down = sub > 0, sub < n_sub - 1
    barrier = pltpu.get_barrier_semaphore()
    for i in range(1, n_shot):
        pl.semaphore_signal(
            barrier, inc=1, device_id={"shot": lax.rem(shot + i, n_shot)}, device_id_type=MESH
        )

    @pl.when(has_up)
    def _():
        pl.semaphore_signal(barrier, inc=1, device_id={"sub": sub - 1}, device_id_type=MESH)

    @pl.when(has_down)
    def _():
        pl.semaphore_signal(barrier, inc=1, device_id={"sub": sub + 1}, device_id_type=MESH)

    beside = jnp.minimum(sub, 1) + jnp.minimum(n_sub - 1 - sub, 1)
    pl.semaphore_wait(barrier, n_shot - 1 + beside)

    def part(i):
        return pl.ds(pl.multiple_of(i * CAP, CAP), CAP)

    copies = []
    for i in range(1, n_shot):
        peer = lax.rem(shot + i, n_shot)
        for src, dst, ss, rs in ((ids_hbm, rids, isend, irecv), (send_hbm, recv, dsend, drecv)):
            copies.append(
                pltpu.make_async_remote_copy(
                    src_ref=src.at[part(peer)], dst_ref=dst.at[CAP * i : CAP * (i + 1)],
                    send_sem=ss.at[i], recv_sem=rs.at[i],
                    device_id={"shot": peer}, device_id_type=MESH,
                )
            )
    for c in copies:
        c.start()
    mine = [
        pltpu.make_async_copy(send_hbm.at[part(shot)], recv.at[0:CAP], lsem.at[0]),
        pltpu.make_async_copy(ids_hbm.at[part(shot)], rids.at[0:CAP], lsem.at[1]),
    ]
    for c in mine:
        c.start()

    band_i = lax.broadcasted_iota(jnp.int32, (depth, 3 * depth), 0)
    band_j = lax.broadcasted_iota(jnp.int32, (depth, 3 * depth), 1) - depth
    there = band_j + sub * depth
    gap = band_i - band_j
    ratio = 2.0 * gap.astype(jnp.float32) / depth
    valid = (jnp.abs(gap) <= depth) & (there >= 0) & (there < n_sub * depth)
    band = jnp.where(valid, jnp.exp(-(ratio * ratio)), 0.0)
    band = band / jnp.sum(band, axis=1, keepdims=True)

    @pl.when(jnp.logical_not(has_up))
    def _():
        tiles[:, 0] = jnp.zeros((TILES_OWN, depth * TX, cols), jnp.float32)

    @pl.when(jnp.logical_not(has_down))
    def _():
        tiles[:, 2] = jnp.zeros((TILES_OWN, depth * TX, cols), jnp.float32)

    def gather(data_ref, id_ref, s, i):
        def layer(z, _):
            rows = pl.ds(pl.multiple_of(z * TX, TX), TX)
            blocks = range(CAP * i, CAP * (i + 1))
            data = [data_ref[p, z] for p in blocks]
            for t in range(TILES_OWN):
                total = tiles[t, s, rows, :] if i else None
                for p, v in zip(blocks, data):
                    term = jnp.where(id_ref[p] == t, v, 0.0)
                    total = term if total is None else total + term
                tiles[t, s, rows, :] = total
            return 0

        lax.fori_loop(0, depth, layer, 0)

    def forwards(i):
        pair = slice(CAP * i, CAP * (i + 1))
        sources = (send_hbm.at[part(shot)], ids_hbm.at[part(shot)]) if i == 0 else (recv.at[pair], rids.at[pair])
        both = []
        for way, peer in ((0, sub - 1), (1, sub + 1)):
            both.append([
                pltpu.make_async_remote_copy(
                    src_ref=source, dst_ref=target.at[way, pair],
                    send_sem=nsend.at[i, way, kind], recv_sem=nrecv.at[i, way, kind],
                    device_id={"sub": peer}, device_id_type=MESH,
                )
                for kind, (source, target) in enumerate(zip(sources, (near, nids)))
            ])
        return both

    def start_forward(i):
        up, down = forwards(i)

        @pl.when(has_up)
        def _():
            for c in up:
                c.start()

        @pl.when(has_down)
        def _():
            for c in down:
                c.start()

    def take_forward(i):
        up, down = forwards(i)

        @pl.when(has_up)
        def _():
            for c in down:
                c.wait_recv()
            gather(near.at[1], nids.at[1], 0, i)

        @pl.when(has_down)
        def _():
            for c in up:
                c.wait_recv()
            gather(near.at[0], nids.at[0], 2, i)

    start_forward(0)
    for c in mine:
        c.wait()
    gather(recv, rids, 1, 0)
    for i in range(1, n_shot):
        copies[2 * i - 2].wait()
        copies[2 * i - 1].wait()
        start_forward(i)
        gather(recv, rids, 1, i)
        take_forward(i - 1)
    take_forward(n_shot - 1)
    for i in range(n_shot):
        up, down = forwards(i)

        @pl.when(has_up)
        def _():
            for c in up:
                c.wait_send()

        @pl.when(has_down)
        def _():
            for c in down:
                c.wait_send()

    def finish(t, _):
        for x in range(TX):
            pencil = jnp.concatenate(
                [tiles[t, s, pl.ds(x, depth, stride=TX), :] for s in range(3)], axis=0
            )
            smooth[t, pl.ds(x, depth, stride=TX), :] = jnp.dot(
                band, pencil, precision=lax.Precision.HIGHEST, preferred_element_type=jnp.float32
            )
        pltpu.make_async_copy(smooth.at[t], out_hbm.at[t], osem.at[t]).start()
        return 0

    lax.fori_loop(0, TILES_OWN, finish, 0)

    def drain(t, _):
        pltpu.make_async_copy(smooth.at[t], out_hbm.at[t], osem.at[t]).wait()
        return 0

    lax.fori_loop(0, TILES_OWN, drain, 0)


def body(courant, adjoint_prev, adjoint_now, forward_accel, traces, receivers, owners, tile_slot):
    n_sub = lax.axis_size("sub")
    n_shot = lax.axis_size("shot")
    _, steps, depth, rows, cols = forward_accel.shape
    places = n_shot * CAP
    f32 = jnp.float32
    smem = pl.BlockSpec(memory_space=pltpu.SMEM)
    vmem = pl.BlockSpec(memory_space=pltpu.VMEM)
    hbm = pl.BlockSpec(memory_space=pl.ANY)

    *source, inverse, ids = pl.pallas_call(
        functools.partial(prepare_kernel, depth * rows * cols, cols),
        out_shape=(
            *[jax.ShapeDtypeStruct((depth * rows, cols), f32)] * steps,
            jax.ShapeDtypeStruct((places,), jnp.int32),
            jax.ShapeDtypeStruct((places, 8, cols), jnp.int32),
        ),
        in_specs=[smem] * 4,
        out_specs=(*[vmem] * steps, smem, vmem),
        scratch_shapes=[pltpu.SMEM((n_shot,), jnp.int32)],
        compiler_params=pltpu.CompilerParams(vmem_limit_bytes=16 * 2**20),
        name="prepare",
    )(receivers, traces, owners, tile_slot)
    source = [field.reshape(depth, rows, cols) for field in source]

    last, send = pl.pallas_call(
        functools.partial(wave_kernel, n_sub),
        out_shape=(
            jax.ShapeDtypeStruct((1, depth, rows, cols), f32),
            jax.ShapeDtypeStruct((places, depth, TX, cols), f32),
        ),
        in_specs=[smem] + [hbm] * 4 + [vmem] * steps,
        out_specs=(hbm, hbm),
        scratch_shapes=[
            pltpu.VMEM((2, depth + 2 * HALO, rows + 2 * PAD, cols), f32),
            pltpu.VMEM((depth, rows, cols), f32),
            pltpu.VMEM((steps, depth, rows, cols), f32),
            pltpu.VMEM((rows // TX, depth, TX, cols), f32),
            pltpu.VMEM((places, depth, TX, cols), f32),
            pltpu.SemaphoreType.DMA((3,)),
            pltpu.SemaphoreType.DMA((steps,)),
            pltpu.SemaphoreType.DMA((steps, 2)),
            pltpu.SemaphoreType.DMA((steps, 2)),
            pltpu.SemaphoreType.DMA((places,)),
            pltpu.SemaphoreType.DMA,
        ],
        compiler_params=pltpu.CompilerParams(
            collective_id=0, has_side_effects=True, vmem_limit_bytes=40 * 2**20
        ),
        name="wave",
    )(inverse, courant, adjoint_prev, adjoint_now, forward_accel, *source)

    smoothed = pl.pallas_call(
        functools.partial(tile_kernel, n_shot, n_sub),
        out_shape=jax.ShapeDtypeStruct((TILES_OWN, depth * TX, cols), f32),
        in_specs=[hbm, hbm],
        out_specs=hbm,
        scratch_shapes=[
            pltpu.VMEM((places, depth, TX, cols), f32),
            pltpu.VMEM((places, 8, cols), jnp.int32),
            pltpu.VMEM((2, places, depth, TX, cols), f32),
            pltpu.VMEM((2, places, 8, cols), jnp.int32),
            pltpu.VMEM((TILES_OWN, 3, depth * TX, cols), f32),
            pltpu.VMEM((TILES_OWN, depth * TX, cols), f32),
            pltpu.SemaphoreType.DMA((2,)),
            pltpu.SemaphoreType.DMA((n_shot,)),
            pltpu.SemaphoreType.DMA((n_shot,)),
            pltpu.SemaphoreType.DMA((n_shot,)),
            pltpu.SemaphoreType.DMA((n_shot,)),
            pltpu.SemaphoreType.DMA((n_shot, 2, 2)),
            pltpu.SemaphoreType.DMA((n_shot, 2, 2)),
            pltpu.SemaphoreType.DMA((TILES_OWN,)),
        ],
        compiler_params=pltpu.CompilerParams(
            collective_id=1, has_side_effects=True, vmem_limit_bytes=32 * 2**20
        ),
        name="tiles",
    )(send, ids)
    return (smoothed.reshape(TILES_OWN, depth, TX, cols), last)


def solution(mesh):
    placed = (
        P("shot", "sub", None, None),
        P("shot", "sub", None, None),
        P("shot", "sub", None, None),
        P("shot", None, "sub", None, None),
        P("shot", None, None),
        P("shot", None),
        P("shot", "sub", None, None),
        P("shot", "sub", None),
    )
    return jax.shard_map(
        body,
        mesh=mesh,
        in_specs=placed,
        out_specs=(P("shot", "sub", None, None), P("shot", "sub", None, None)),
        check_vma=False,
    )
```

```python
import functools

import jax
import jax.numpy as jnp
from jax import lax
from jax.experimental import pallas as pl
from jax.experimental.pallas import tpu as pltpu
from jax.sharding import PartitionSpec as P

TX = 8
TILES_OWN = 8
CAP = 2
HALO = 4
PAD = 8
MESH = pl.DeviceIdType.MESH

stencil_weights = (-205.0 / 72.0, 8.0 / 5.0, -1.0 / 5.0, 8.0 / 315.0, -1.0 / 560.0)


def prepare_kernel(slab_cells, cols_y, rec_ref, tr_ref, own_ref, slot_ref, src_ref, inv_ref, ids_ref, count_ref):
    steps = src_ref.shape[0]
    zrows = 256

    def zero(i, _):
        src_ref[:, pl.ds(pl.multiple_of(i * zrows, zrows), zrows), :] = jnp.zeros(
            (steps, zrows, cols_y), jnp.float32
        )
        return 0

    lax.fori_loop(0, src_ref.shape[1] // zrows, zero, 0)
    base = lax.axis_index("sub") * slab_cells
    lane = lax.broadcasted_iota(jnp.int32, (1, cols_y), 1)

    def add(r, _):
        off = rec_ref[0, r] - base

        @pl.when((off >= 0) & (off < slab_cells))
        def _():
            row = lax.div(off, cols_y)
            hit = lane == lax.rem(off, cols_y)
            for t in range(steps):
                src_ref[t, pl.ds(row, 1), :] += jnp.where(hit, tr_ref[0, t, r], 0.0)

        return 0

    lax.fori_loop(0, rec_ref.shape[1], add, 0, unroll=4)

    ids_ref[...] = jnp.full(ids_ref.shape, -1, jnp.int32)
    for i in range(count_ref.shape[0]):
        count_ref[i] = 0
    for i in range(inv_ref.shape[0]):
        inv_ref[i] = 0
    for k in range(slot_ref.shape[2]):
        owner = own_ref[0, 0, k, 0]
        place = owner * CAP + count_ref[owner]
        count_ref[owner] = count_ref[owner] + 1
        inv_ref[place] = k
        ids_ref[pl.ds(place, 1)] = jnp.full((1,) + ids_ref.shape[1:], slot_ref[0, 0, k], jnp.int32)


def wave_kernel(
    n_sub, inv_ref, cour_hbm, prev_hbm, now_hbm, acc_hbm, src_hbm,
    last_hbm, send_hbm,
    even, odd, cour, acc, src, grad, packed,
    lsem, tsem, hsend, hrecv, psem, osem,
):
    buf = (even, odd)
    me = lax.axis_index("sub")
    steps, depth, rows, cols = acc.shape
    lo, hi = HALO, HALO + depth
    inner = pl.ds(PAD, rows)

    local = [
        pltpu.make_async_copy(now_hbm.at[0], even.at[lo:hi, inner, :], lsem.at[0]),
        pltpu.make_async_copy(prev_hbm.at[0], odd.at[lo:hi, inner, :], lsem.at[1]),
        pltpu.make_async_copy(cour_hbm.at[0], cour, lsem.at[2]),
    ]
    per_step = [
        (
            pltpu.make_async_copy(src_hbm.at[t], src.at[t], tsem.at[t, 0]),
            pltpu.make_async_copy(acc_hbm.at[0, t], acc.at[t], tsem.at[t, 1]),
        )
        for t in range(steps)
    ]
    for c in local:
        c.start()
    for t in range(steps):
        for c in per_step[t]:
            c.start()

    for ref in buf:
        ref[:, 0:PAD, :] = jnp.zeros((depth + 2 * HALO, PAD, cols), jnp.float32)
        ref[:, PAD + rows :, :] = jnp.zeros((depth + 2 * HALO, PAD, cols), jnp.float32)
        ref[0:lo, inner, :] = jnp.zeros((HALO, rows, cols), jnp.float32)
        ref[hi:, inner, :] = jnp.zeros((HALO, rows, cols), jnp.float32)

    has_up, has_down = me > 0, me < n_sub - 1
    barrier = pltpu.get_barrier_semaphore()

    @pl.when(has_up)
    def _():
        pl.semaphore_signal(barrier, inc=1, device_id={"sub": me - 1}, device_id_type=MESH)

    @pl.when(has_down)
    def _():
        pl.semaphore_signal(barrier, inc=1, device_id={"sub": me + 1}, device_id_type=MESH)

    pl.semaphore_wait(barrier, jnp.minimum(me, 1) + jnp.minimum(n_sub - 1 - me, 1))

    def halos(t):
        b = t % 2
        if t == 0:
            first, final = now_hbm.at[0, 0:HALO], now_hbm.at[0, depth - HALO : depth]
        else:
            first = buf[b].at[lo : lo + HALO, inner, :]
            final = buf[b].at[hi - HALO : hi, inner, :]
        up = pltpu.make_async_remote_copy(
            src_ref=first, dst_ref=buf[b].at[hi : hi + HALO, inner, :],
            send_sem=hsend.at[t, 0], recv_sem=hrecv.at[t, 0],
            device_id={"sub": me - 1}, device_id_type=MESH,
        )
        down = pltpu.make_async_remote_copy(
            src_ref=final, dst_ref=buf[b].at[0:HALO, inner, :],
            send_sem=hsend.at[t, 1], recv_sem=hrecv.at[t, 1],
            device_id={"sub": me + 1}, device_id_type=MESH,
        )
        return up, down

    def start_halos(t):
        up, down = halos(t)

        @pl.when(has_up)
        def _():
            up.start()

        @pl.when(has_down)
        def _():
            down.start()

    def wait_halos(t):
        up, down = halos(t)

        @pl.when(has_up)
        def _():
            up.wait_send()
            down.wait_recv()

        @pl.when(has_down)
        def _():
            down.wait_send()
            up.wait_recv()

    start_halos(0)

    lane = lax.broadcasted_iota(jnp.int32, (TX, cols), 1)
    from_left = [None] + [jnp.where(lane >= d, stencil_weights[d], 0.0) for d in range(1, 5)]
    from_right = [None] + [jnp.where(lane < cols - d, stencil_weights[d], 0.0) for d in range(1, 5)]

    def advance(t, chunks):
        cur, nxt = buf[t % 2], buf[(t + 1) % 2]

        def block(xb, _):
            x0 = pl.multiple_of(xb * TX, TX)
            own = pl.ds(x0, TX)
            here = pl.ds(pl.multiple_of(x0 + PAD, TX), TX)
            for za, zb in chunks:
                col = {z: cur[z + HALO, here, :] for z in range(za - 4, zb + 4)}
                done = []
                for z in range(za, zb):
                    c = col[z]
                    lap = (3.0 * stencil_weights[0]) * c
                    for d in range(1, 5):
                        pair = (col[z + d] + col[z - d]) + (
                            cur[z + HALO, pl.ds(x0 + (PAD + d), TX), :]
                            + cur[z + HALO, pl.ds(x0 + (PAD - d), TX), :]
                        )
                        lap = lap + stencil_weights[d] * pair
                        lap = lap + from_left[d] * pltpu.roll(c, d, 1)
                        lap = lap + from_right[d] * pltpu.roll(c, cols - d, 1)
                    adv = (2.0 * c - nxt[z + HALO, here, :]) + (
                        cour[z, own, :] * lap + src[t, z, own, :]
                    )
                    done.append(adv)
                for z, adv in zip(range(za, zb), done):
                    nxt[z + HALO, here, :] = adv
                    g = adv * acc[t, z, own, :]
                    grad[xb, z] = g if t == 0 else grad[xb, z] + g
            return 0

        lax.fori_loop(0, rows // TX, block, 0)

    for c in local:
        c.wait()
    mid = [(z, min(z + 8, depth - HALO)) for z in range(HALO, depth - HALO, 8)]
    for t in range(steps):
        for c in per_step[t]:
            c.wait()
        advance(t, mid)
        wait_halos(t)
        advance(t, [(0, HALO), (depth - HALO, depth)])
        if t + 1 < steps:
            start_halos(t + 1)

    out = pltpu.make_async_copy(buf[steps % 2].at[lo:hi, inner, :], last_hbm.at[0], osem)
    out.start()
    places = packed.shape[0]

    def pack(p, _):
        packed[p] = grad[inv_ref[p]]
        pltpu.make_async_copy(packed.at[p], send_hbm.at[p], psem.at[p]).start()
        return 0

    lax.fori_loop(0, places, pack, 0)

    def drain(p, _):
        pltpu.make_async_copy(packed.at[p], send_hbm.at[p], psem.at[p]).wait()
        return 0

    lax.fori_loop(0, places, drain, 0)
    out.wait()


def tile_kernel(
    n_shot, n_sub, send_hbm, ids_hbm, out_hbm,
    recv, rids, tiles, smooth,
    lsem, dsend, drecv, isend, irecv, nsend, nrecv, osem,
):
    shot, sub = lax.axis_index("shot"), lax.axis_index("sub")
    depth, cols = recv.shape[1], recv.shape[3]
    has_up, has_down = sub > 0, sub < n_sub - 1
    barrier = pltpu.get_barrier_semaphore()
    for i in range(1, n_shot):
        pl.semaphore_signal(
            barrier, inc=1, device_id={"shot": lax.rem(shot + i, n_shot)}, device_id_type=MESH
        )

    @pl.when(has_up)
    def _():
        pl.semaphore_signal(barrier, inc=1, device_id={"sub": sub - 1}, device_id_type=MESH)

    @pl.when(has_down)
    def _():
        pl.semaphore_signal(barrier, inc=1, device_id={"sub": sub + 1}, device_id_type=MESH)

    near = jnp.minimum(sub, 1) + jnp.minimum(n_sub - 1 - sub, 1)
    pl.semaphore_wait(barrier, n_shot - 1 + near)

    def part(i):
        return pl.ds(pl.multiple_of(i * CAP, CAP), CAP)

    copies = []
    for i in range(1, n_shot):
        peer = lax.rem(shot + i, n_shot)
        for src, dst, ss, rs in ((ids_hbm, rids, isend, irecv), (send_hbm, recv, dsend, drecv)):
            copies.append(
                pltpu.make_async_remote_copy(
                    src_ref=src.at[part(peer)], dst_ref=dst.at[CAP * i : CAP * (i + 1)],
                    send_sem=ss.at[i], recv_sem=rs.at[i],
                    device_id={"shot": peer}, device_id_type=MESH,
                )
            )
    for c in copies:
        c.start()
    mine = [
        pltpu.make_async_copy(send_hbm.at[part(shot)], recv.at[0:CAP], lsem.at[0]),
        pltpu.make_async_copy(ids_hbm.at[part(shot)], rids.at[0:CAP], lsem.at[1]),
    ]
    for c in mine:
        c.start()

    band_i = lax.broadcasted_iota(jnp.int32, (depth, 3 * depth), 0)
    band_j = lax.broadcasted_iota(jnp.int32, (depth, 3 * depth), 1) - depth
    there = band_j + sub * depth
    gap = band_i - band_j
    ratio = 2.0 * gap.astype(jnp.float32) / depth
    valid = (jnp.abs(gap) <= depth) & (there >= 0) & (there < n_sub * depth)
    band = jnp.where(valid, jnp.exp(-(ratio * ratio)), 0.0)
    band = band / jnp.sum(band, axis=1, keepdims=True)

    @pl.when(jnp.logical_not(has_up))
    def _():
        tiles[:, 0] = jnp.zeros((TILES_OWN, depth * TX, cols), jnp.float32)

    @pl.when(jnp.logical_not(has_down))
    def _():
        tiles[:, 2] = jnp.zeros((TILES_OWN, depth * TX, cols), jnp.float32)

    def gather(blocks, fresh):
        def layer(z, _):
            rows = pl.ds(pl.multiple_of(z * TX, TX), TX)
            data = [recv[p, z] for p in blocks]
            for t in range(TILES_OWN):
                total = None if fresh else tiles[t, 1, rows, :]
                for p, v in zip(blocks, data):
                    term = jnp.where(rids[p] == t, v, 0.0)
                    total = term if total is None else total + term
                tiles[t, 1, rows, :] = total
            return 0

        lax.fori_loop(0, depth, layer, 0)

    for c in mine:
        c.wait()
    gather(range(CAP), True)
    for i in range(1, n_shot):
        copies[2 * i - 2].wait()
        copies[2 * i - 1].wait()
        gather(range(CAP * i, CAP * (i + 1)), False)

    def edge(t):
        up = pltpu.make_async_remote_copy(
            src_ref=tiles.at[t, 1], dst_ref=tiles.at[t, 2],
            send_sem=nsend.at[t, 0], recv_sem=nrecv.at[t, 0],
            device_id={"sub": sub - 1}, device_id_type=MESH,
        )
        down = pltpu.make_async_remote_copy(
            src_ref=tiles.at[t, 1], dst_ref=tiles.at[t, 0],
            send_sem=nsend.at[t, 1], recv_sem=nrecv.at[t, 1],
            device_id={"sub": sub + 1}, device_id_type=MESH,
        )
        return up, down

    def start_edge(t, _):
        up, down = edge(t)

        @pl.when(has_up)
        def _():
            up.start()

        @pl.when(has_down)
        def _():
            down.start()

        return 0

    lax.fori_loop(0, TILES_OWN, start_edge, 0)

    def finish(t, _):
        up, down = edge(t)

        @pl.when(has_up)
        def _():
            up.wait_send()
            down.wait_recv()

        @pl.when(has_down)
        def _():
            down.wait_send()
            up.wait_recv()

        for x in range(TX):
            pencil = jnp.concatenate(
                [tiles[t, s, pl.ds(x, depth, stride=TX), :] for s in range(3)], axis=0
            )
            smooth[t, pl.ds(x, depth, stride=TX), :] = jnp.dot(
                band, pencil, precision=lax.Precision.HIGHEST, preferred_element_type=jnp.float32
            )
        pltpu.make_async_copy(smooth.at[t], out_hbm.at[t], osem.at[t]).start()
        return 0

    lax.fori_loop(0, TILES_OWN, finish, 0)

    def drain(t, _):
        pltpu.make_async_copy(smooth.at[t], out_hbm.at[t], osem.at[t]).wait()
        return 0

    lax.fori_loop(0, TILES_OWN, drain, 0)


def body(courant, adjoint_prev, adjoint_now, forward_accel, traces, receivers, owners, tile_slot):
    n_sub = lax.axis_size("sub")
    n_shot = lax.axis_size("shot")
    _, steps, depth, rows, cols = forward_accel.shape
    places = n_shot * CAP
    f32 = jnp.float32
    smem = pl.BlockSpec(memory_space=pltpu.SMEM)
    vmem = pl.BlockSpec(memory_space=pltpu.VMEM)
    hbm = pl.BlockSpec(memory_space=pl.ANY)

    source, inverse, ids = pl.pallas_call(
        functools.partial(prepare_kernel, depth * rows * cols, cols),
        out_shape=(
            jax.ShapeDtypeStruct((steps, depth * rows, cols), f32),
            jax.ShapeDtypeStruct((places,), jnp.int32),
            jax.ShapeDtypeStruct((places, 8, cols), jnp.int32),
        ),
        in_specs=[smem] * 4,
        out_specs=(vmem, smem, vmem),
        scratch_shapes=[pltpu.SMEM((n_shot,), jnp.int32)],
        compiler_params=pltpu.CompilerParams(vmem_limit_bytes=32 * 2**20),
        name="prepare",
    )(receivers, traces, owners, tile_slot)
    source = source.reshape(steps, depth, rows, cols)

    last, send = pl.pallas_call(
        functools.partial(wave_kernel, n_sub),
        out_shape=(
            jax.ShapeDtypeStruct((1, depth, rows, cols), f32),
            jax.ShapeDtypeStruct((places, depth, TX, cols), f32),
        ),
        in_specs=[smem] + [hbm] * 5,
        out_specs=(hbm, hbm),
        scratch_shapes=[
            pltpu.VMEM((depth + 2 * HALO, rows + 2 * PAD, cols), f32),
            pltpu.VMEM((depth + 2 * HALO, rows + 2 * PAD, cols), f32),
            pltpu.VMEM((depth, rows, cols), f32),
            pltpu.VMEM((steps, depth, rows, cols), f32),
            pltpu.VMEM((steps, depth, rows, cols), f32),
            pltpu.VMEM((rows // TX, depth, TX, cols), f32),
            pltpu.VMEM((places, depth, TX, cols), f32),
            pltpu.SemaphoreType.DMA((3,)),
            pltpu.SemaphoreType.DMA((steps, 2)),
            pltpu.SemaphoreType.DMA((steps, 2)),
            pltpu.SemaphoreType.DMA((steps, 2)),
            pltpu.SemaphoreType.DMA((places,)),
            pltpu.SemaphoreType.DMA,
        ],
        compiler_params=pltpu.CompilerParams(
            collective_id=0, has_side_effects=True, vmem_limit_bytes=48 * 2**20
        ),
        name="wave",
    )(inverse, courant, adjoint_prev, adjoint_now, forward_accel, source)

    smoothed = pl.pallas_call(
        functools.partial(tile_kernel, n_shot, n_sub),
        out_shape=jax.ShapeDtypeStruct((TILES_OWN, depth * TX, cols), f32),
        in_specs=[hbm, hbm],
        out_specs=hbm,
        scratch_shapes=[
            pltpu.VMEM((places, depth, TX, cols), f32),
            pltpu.VMEM((places, 8, cols), jnp.int32),
            pltpu.VMEM((TILES_OWN, 3, depth * TX, cols), f32),
            pltpu.VMEM((TILES_OWN, depth * TX, cols), f32),
            pltpu.SemaphoreType.DMA((2,)),
            pltpu.SemaphoreType.DMA((n_shot,)),
            pltpu.SemaphoreType.DMA((n_shot,)),
            pltpu.SemaphoreType.DMA((n_shot,)),
            pltpu.SemaphoreType.DMA((n_shot,)),
            pltpu.SemaphoreType.DMA((TILES_OWN, 2)),
            pltpu.SemaphoreType.DMA((TILES_OWN, 2)),
            pltpu.SemaphoreType.DMA((TILES_OWN,)),
        ],
        compiler_params=pltpu.CompilerParams(
            collective_id=1, has_side_effects=True, vmem_limit_bytes=32 * 2**20
        ),
        name="tiles",
    )(send, ids)
    return (smoothed.reshape(TILES_OWN, depth, TX, cols), last)


def solution(mesh):
    placed = (
        P("shot", "sub", None, None),
        P("shot", "sub", None, None),
        P("shot", "sub", None, None),
        P("shot", None, "sub", None, None),
        P("shot", None, None),
        P("shot", None),
        P("shot", "sub", None, None),
        P("shot", "sub", None),
    )
    return jax.shard_map(
        body,
        mesh=mesh,
        in_specs=placed,
        out_specs=(P("shot", "sub", None, None), P("shot", "sub", None, None)),
        check_vma=False,
    )
```
